32 devices in a mesh: lat: 4 (over z), gx: 2 (over y), gy: 4 (over x, core).
Axes of the slice: x: 2, y: 2, z: 4, core: 2. Of those that a mesh axis runs over, the one named last changes fastest.
Arguments:
- latents: bfloat16 [256, 1024], P(('lat', 'gx', 'gy')), may hold values from -16 to 16
- w_key: bfloat16 [1024, 128], replicated, may hold values from -0.375 to 0.375
- w_value: bfloat16 [1024, 128], replicated, may hold values from -0.1875 to 0.1875
- queries: bfloat16 [64, 64, 8, 128], P(('lat', 'gx'), 'gy'), may hold values from -15 to 15
- conv_one: bfloat16 [3, 3, 64, 384], replicated, may hold values from -0.109375 to 0.109375
- bias_one: float32 [64], replicated, may hold values from -2.5 to 2.5
- conv_two: bfloat16 [3, 3, 64, 192], replicated, may hold values from -0.15625 to 0.15625
- bias_two: float32 [64], replicated, may hold values from -2.5 to 2.5
Outputs:
- voxel_out: bfloat16 [64, 64, 512], P(('lat', 'gx'), 'gy')
The draws below stay inside these ranges and needn't reach their ends.
All inputs are finite; a program needn't handle non-finite values.
Results may differ from the reference program's by a relative error of at most 0.0097.
Values may be sent and summed in bfloat16 or wider, within the bound.
A program may use at most 64 MiB of HBM per device.

```python
import math
import jax
import jax.numpy as jnp
from jax import lax

DL = 1024
DH = 128
C1 = 64
SLAB = 8
NL = 256
NXV = 64
NYV = 64


def draw_w_key(key, part):
    base = jax.random.normal(jax.random.fold_in(key, 1), (DL, DH), jnp.float32) / math.sqrt(DL)
    base = jnp.clip(base, -0.375, 0.375)
    return base.astype(jnp.bfloat16)


def draw_latents(key, part):
    base = jnp.clip(jax.random.normal(jax.random.fold_in(key, 3), (NL, DL), jnp.float32), -6.0, 6.0)
    return base.astype(jnp.bfloat16)


def draw_queries(key, part):
    shape_all = (NXV, NYV, SLAB, DH)
    base = jnp.clip(2.5 * jax.random.normal(jax.random.fold_in(key, 5), shape_all, jnp.float32), -15.0, 15.0)
    return base.astype(jnp.bfloat16)


def normal_values(key, dims, scale, most, held_as=jnp.bfloat16):
    entries = jax.random.normal(key, dims, jnp.float32) * scale
    return jnp.minimum(jnp.maximum(entries, -most), most).astype(held_as)


def setup_inputs(seed: int = 0) -> dict:
    splits = jax.random.split(jax.random.key(seed), 9)
    latents = draw_latents(jax.random.fold_in(splits[8], 71), 0)
    w_key = draw_w_key(jax.random.fold_in(splits[8], 71), 0)
    w_value = normal_values(splits[2], (DL, DH), DL ** -0.5, 0.1875)
    queries = draw_queries(jax.random.fold_in(splits[8], 71), 0)
    conv_one = normal_values(splits[4], (3, 3, C1, 3 * DH), (27 * DH) ** -0.5, 0.109375)
    bias_one = normal_values(splits[5], (C1,), 0.5, 2.5, jnp.float32)
    conv_two = normal_values(splits[6], (3, 3, C1, 3 * C1), (27 * C1) ** -0.5, 0.15625)
    bias_two = normal_values(splits[7], (C1,), 0.5, 2.5, jnp.float32)
    return {"latents": latents, "w_key": w_key, "w_value": w_value, "queries": queries, "conv_one": conv_one, "bias_one": bias_one, "conv_two": conv_two, "bias_two": bias_two}


def convolve_grid(volume, kernel, out_channels, in_channels):
    kernel_full = kernel.astype(jnp.float32).reshape(3, 3, out_channels, 3, in_channels).transpose(0, 1, 3, 4, 2)
    result = lax.conv_general_dilated(volume[None].astype(jnp.float32), kernel_full, (1, 1, 1), 'SAME', dimension_numbers=('NDHWC', 'DHWIO', 'NDHWC'), precision=lax.Precision.HIGHEST, preferred_element_type=jnp.float32)
    return result[0]

def reference(latents, w_key, w_value, queries, conv_one, bias_one, conv_two, bias_two):
    key_rows = jnp.dot(latents, w_key, preferred_element_type=jnp.float32).astype(jnp.bfloat16)
    value_rows = jnp.dot(latents, w_value, preferred_element_type=jnp.float32).astype(jnp.bfloat16)
    value_wide = value_rows.astype(jnp.float32)
    score_scale = 1.0 / math.sqrt(DH)
    voxel_count = NXV * NYV * SLAB
    block_rows = math.gcd(voxel_count, 512)
    query_blocks = queries.reshape(voxel_count // block_rows, block_rows, DH)

    def attend_block(query_rows):
        scores = lax.dot_general(query_rows, key_rows, (((1,), (1,)), ((), ())), preferred_element_type=jnp.float32) * score_scale
        row_max = lax.optimization_barrier(jnp.max(scores, axis=1, keepdims=True))
        weights = jnp.exp(scores - row_max)
        denominator = lax.optimization_barrier(jnp.sum(weights, axis=1, keepdims=True))
        mixed = jnp.dot(weights, value_wide, precision=lax.Precision.HIGHEST, preferred_element_type=jnp.float32)
        return mixed / denominator
    attended = lax.map(attend_block, query_blocks).reshape(NXV, NYV, SLAB, DH).astype(jnp.bfloat16)
    pre_act = convolve_grid(attended, conv_one, C1, DH) + bias_one
    hidden = jax.nn.silu(pre_act).astype(jnp.bfloat16)
    final = convolve_grid(hidden, conv_two, C1, C1) + bias_two
    return final.reshape(NXV, NYV, SLAB * C1).astype(jnp.bfloat16)
```

```python
from functools import partial
import math

import jax
import jax.numpy as jnp
from jax import lax
from jax.experimental import pallas as pl
from jax.experimental.pallas import tpu as pltpu
from jax.sharding import PartitionSpec as P

MESH = pl.DeviceIdType.MESH
DIRECTIONS = [(dx, dy) for dx in (-1, 0, 1) for dy in (-1, 0, 1) if (dx, dy) != (0, 0)]
BF16 = jnp.bfloat16
F32 = jnp.float32
NT = (((1,), (1,)), ((), ()))


def kernel(
    sizes, latents, w_key, w_value, queries, conv_one, bias_one, conv_two, bias_two, out,
    latents_v, wk_v, wv_v, q_pad, c1_v, b1_v, c2_v, b2_v, kv, att3, hid3, result,
    local_sem, halo_send, halo_recv, col_send, col_recv, plane_send, plane_recv, keys, values,
):
    n_lat, n_gx, n_gy, rows, cols, slab = sizes
    lat, gx, gy = lax.axis_index("lat"), lax.axis_index("gx"), lax.axis_index("gy")
    n_plane = n_gx * n_gy
    plane = gx * n_gy + gy
    n_row_tiles = n_lat * n_gx
    row_tile = lat * n_gx + gx
    wide = cols * slab
    edge = 2 * slab

    def device_of(tile_x, tile_y):
        return (tile_x // n_gx, tile_x % n_gx, tile_y)

    def present(tile_x, tile_y):
        return (tile_x >= 0) & (tile_x < n_row_tiles) & (tile_y >= 0) & (tile_y < n_gy)

    def plane_device(index):
        return (lat, index // n_gy, index % n_gy)

    loads = [
        pltpu.make_async_copy(src, dst, local_sem.at[i])
        for i, (src, dst) in enumerate([
            (latents, latents_v),
            (w_key, wk_v),
            (w_value, wv_v),
            (queries, q_pad.at[pl.ds(2, rows), pl.ds(edge, wide)]),
            (conv_one, c1_v),
            (bias_one, b1_v),
            (conv_two, c2_v),
            (bias_two, b2_v),
        ])
    ]
    for load in loads:
        load.start()

    barrier = pltpu.get_barrier_semaphore()
    awaited = n_lat - 1 + n_plane - 1
    for k in range(1, n_lat):
        pl.semaphore_signal(barrier, inc=1, device_id=((lat + k) % n_lat, gx, gy), device_id_type=MESH)
    for k in range(1, n_plane):
        pl.semaphore_signal(barrier, inc=1, device_id=plane_device((plane + k) % n_plane), device_id_type=MESH)
    for dx, dy in DIRECTIONS:
        there = present(row_tile + dx, gy + dy)
        awaited = awaited + there.astype(jnp.int32)

        @pl.when(there)
        def _():
            pl.semaphore_signal(
                barrier, inc=1, device_id=device_of(row_tile + dx, gy + dy), device_id_type=MESH
            )

    for load in loads[:3]:
        load.wait()
    lat_rows = latents_v[...]
    key_rows = jnp.dot(lat_rows, wk_v[...], preferred_element_type=F32).astype(BF16)
    value_rows = jnp.dot(lat_rows, wv_v[...], preferred_element_type=F32).astype(BF16)
    kv[plane, lat] = jnp.concatenate([key_rows, value_rows], axis=1)

    pl.semaphore_wait(barrier, awaited)

    def column_copy(k, owner):
        slot = kv.at[plane, owner]
        return pltpu.make_async_remote_copy(
            src_ref=slot, dst_ref=slot, send_sem=col_send.at[k], recv_sem=col_recv.at[k],
            device_id=((lat + k) % n_lat, gx, gy), device_id_type=MESH,
        )

    def plane_copy(k, owner):
        slot = kv.at[owner]
        return pltpu.make_async_remote_copy(
            src_ref=slot, dst_ref=slot, send_sem=plane_send.at[k], recv_sem=plane_recv.at[k],
            device_id=plane_device((plane + k) % n_plane), device_id_type=MESH,
        )

    def halo_copy(i, dx, dy):
        src_x = {1: rows - 2, -1: 0, 0: 0}[dx]
        dst_x = {1: 0, -1: rows + 2, 0: 2}[dx]
        src_y = {1: wide - edge, -1: 0, 0: 0}[dy]
        dst_y = {1: 0, -1: wide + edge, 0: edge}[dy]
        size_x, size_y = (rows if dx == 0 else 2), (wide if dy == 0 else edge)
        return pltpu.make_async_remote_copy(
            src_ref=queries.at[pl.ds(src_x, size_x), pl.ds(src_y, size_y)],
            dst_ref=q_pad.at[pl.ds(dst_x, size_x), pl.ds(dst_y, size_y)],
            send_sem=halo_send.at[i], recv_sem=halo_recv.at[i],
            device_id=device_of(row_tile + dx, gy + dy), device_id_type=MESH,
        )

    for k in range(1, n_lat):
        column_copy(k, lat).start()
    for i, (dx, dy) in enumerate(DIRECTIONS):
        @pl.when(present(row_tile + dx, gy + dy))
        def _():
            halo_copy(i, dx, dy).start()

    for k in range(1, n_lat):
        column_copy(k, (lat + n_lat - k) % n_lat).wait_recv()
    for k in range(1, n_plane):
        plane_copy(k, plane).start()

    for load in loads[3:]:
        load.wait()
    for i, (dx, dy) in enumerate(DIRECTIONS):
        @pl.when(present(row_tile - dx, gy - dy))
        def _():
            halo_copy(i, dx, dy).wait_recv()

    for k in range(1, n_plane):
        plane_copy(k, (plane + n_plane - k) % n_plane).wait_recv()

    n_all = n_plane * n_lat * kv.shape[2]
    channels = q_pad.shape[2]
    block = min(n_all, 256)
    piece_planes = block // (n_lat * kv.shape[2])
    for first in range(0, n_plane, piece_planes):
        every = kv[pl.ds(first, piece_planes)].reshape(block, 2 * channels)
        spot = pl.ds(first * n_lat * kv.shape[2], block)
        keys[spot, :] = every[:, :channels]
        values[spot, :channels] = every[:, channels:]
        values[spot, channels:] = jnp.ones((block, channels), BF16)
    exponent_scale = math.log2(math.e) / math.sqrt(channels)
    padded = wide + 2 * edge

    def shifted(cells):
        level = lax.broadcasted_iota(jnp.int32, cells.shape, 1)
        below = jnp.where(level == 0, 0.0, pltpu.roll(cells, 1, 1))
        above = jnp.where(level == slab - 1, 0.0, pltpu.roll(cells, slab - 1, 1))
        return below, above

    def attend(first, count):
        q = q_pad[pl.ds(first, count)].reshape(count * padded, channels)

        def fold(first_latent, state):
            spot = pl.ds(first_latent, block)
            scores = lax.dot_general(q, keys[spot, :], NT, preferred_element_type=F32)
            top = jnp.max(scores, axis=1, keepdims=True)
            if state is not None:
                top = jnp.maximum(top, state[0])
            weights = jnp.exp2((scores - top) * exponent_scale).astype(BF16)
            mixed = jnp.dot(weights, values[spot, :], preferred_element_type=F32)
            if state is not None:
                mixed = mixed + state[1] * jnp.exp2((state[0] - top) * exponent_scale)
            return top, mixed

        state = fold(0, None)
        if n_all > block:
            state = lax.fori_loop(
                1, n_all // block, lambda i, held: fold(pl.multiple_of(i * block, block), held), state
            )
        mixed = state[1]
        cells = (mixed[:, :channels] / mixed[:, channels:]).reshape(-1, slab, channels)
        below, above = shifted(cells)
        for c, part in enumerate((below, cells, above)):
            att3[pl.ds(first, count), :, c * channels : (c + 1) * channels] = (
                part.astype(BF16).reshape(count, padded, channels)
            )

    step = max(1, min(4, 1024 // n_all))
    steps = (rows + 4) // step
    if steps <= 4:
        for s in range(steps):
            attend(s * step, step)
    else:
        @pl.loop(0, steps)
        def _(s):
            attend(s * step, step)

    def blank(when, ref, index):
        @pl.when(when)
        def _():
            view = ref.at[index]
            view[...] = jnp.zeros(view.shape, ref.dtype)

    every_dim = slice(None)
    blank(row_tile == 0, att3, (pl.ds(0, 2), every_dim, every_dim))
    blank(row_tile == n_row_tiles - 1, att3, (pl.ds(rows + 2, 2), every_dim, every_dim))
    blank(gy == 0, att3, (every_dim, pl.ds(0, edge), every_dim))
    blank(gy == n_gy - 1, att3, (every_dim, pl.ds(wide + edge, edge), every_dim))

    def convolve(ref, weight, first, count, mid):
        length = ref.shape[1]
        total = None
        for a in range(3):
            cells = ref[pl.ds(first + a, count)].reshape(count * length, ref.shape[2])
            term = lax.dot_general(cells, weight[a], NT, preferred_element_type=F32)
            total = term if total is None else total + term
        total = total.reshape(count, length, 3 * mid)
        kept = length - 2 * slab
        return (
            total[:, :kept, :mid]
            + total[:, slab : slab + kept, mid : 2 * mid]
            + total[:, 2 * slab :, 2 * mid :]
        )

    mid = b1_v.shape[1]
    for first in range(0, rows + 2, 5):
        count = min(5, rows + 2 - first)
        half = (convolve(att3, c1_v, first, count, mid) + b1_v[...]) * 0.5
        cells = (half + half * jnp.tanh(half)).reshape(-1, slab, mid)
        below, above = shifted(cells)
        stacked = jnp.concatenate([below, cells, above], axis=2).astype(BF16)
        hid3[pl.ds(first, count)] = stacked.reshape(count, wide + edge, 3 * mid)

    blank(row_tile == 0, hid3, (pl.ds(0, 1), every_dim, every_dim))
    blank(row_tile == n_row_tiles - 1, hid3, (pl.ds(rows + 1, 1), every_dim, every_dim))
    blank(gy == 0, hid3, (every_dim, pl.ds(0, slab), every_dim))
    blank(gy == n_gy - 1, hid3, (every_dim, pl.ds(wide + slab, slab), every_dim))

    for first in range(0, rows, 4):
        final = convolve(hid3, c2_v, first, 4, mid) + b2_v[...]
        result[pl.ds(first * wide, 4 * wide), :mid] = final.reshape(4 * wide, mid)
    pieces = [result[pl.ds(z, rows * cols, stride=slab), :][:, :mid] for z in range(slab)]
    out[...] = jnp.concatenate(pieces, axis=1).astype(BF16)

    for k in range(1, n_lat):
        column_copy(k, lat).wait_send()
    for k in range(1, n_plane):
        plane_copy(k, plane).wait_send()
    for i, (dx, dy) in enumerate(DIRECTIONS):
        @pl.when(present(row_tile + dx, gy + dy))
        def _():
            halo_copy(i, dx, dy).wait_send()


def shards(sizes, latents, w_key, w_value, queries, conv_one, bias_one, conv_two, bias_two):
    rows, cols, slab, channels = queries.shape
    mid = conv_one.shape[2]
    n_lat, n_gx, n_gy = sizes
    piece = latents.shape[0]
    n_plane = n_gx * n_gy
    any_spec = pl.BlockSpec(memory_space=pl.ANY)
    operands = (
        latents, w_key, w_value,
        queries.reshape(rows, cols * slab, channels),
        conv_one.reshape(3, 3 * mid, 3 * channels),
        bias_one.reshape(1, mid),
        conv_two.reshape(3, 3 * mid, 3 * mid),
        bias_two.reshape(1, mid),
    )
    result = pl.pallas_call(
        partial(kernel, (n_lat, n_gx, n_gy, rows, cols, slab)),
        out_shape=jax.ShapeDtypeStruct((rows * cols, slab * mid), BF16),
        in_specs=[any_spec] * 8,
        out_specs=pl.BlockSpec(memory_space=pltpu.VMEM),
        scratch_shapes=[
            pltpu.VMEM(latents.shape, BF16),
            pltpu.VMEM(w_key.shape, BF16),
            pltpu.VMEM(w_value.shape, BF16),
            pltpu.VMEM((rows + 4, (cols + 4) * slab, channels), BF16),
            pltpu.VMEM(operands[4].shape, BF16),
            pltpu.VMEM((1, mid), F32),
            pltpu.VMEM(operands[6].shape, BF16),
            pltpu.VMEM((1, mid), F32),
            pltpu.VMEM((n_plane, n_lat, piece, 2 * channels), BF16),
            pltpu.VMEM((rows + 4, (cols + 4) * slab, 3 * channels), BF16),
            pltpu.VMEM((rows + 2, (cols + 2) * slab, 3 * mid), BF16),
            pltpu.VMEM((rows * cols * slab, 2 * mid), F32),
            pltpu.SemaphoreType.DMA((8,)),
            pltpu.SemaphoreType.DMA((8,)),
            pltpu.SemaphoreType.DMA((8,)),
            pltpu.SemaphoreType.DMA((n_lat,)),
            pltpu.SemaphoreType.DMA((n_lat,)),
            pltpu.SemaphoreType.DMA((n_plane,)),
            pltpu.SemaphoreType.DMA((n_plane,)),
            pltpu.VMEM((n_plane * n_lat * piece, channels), BF16),
            pltpu.VMEM((n_plane * n_lat * piece, 2 * channels), BF16),
        ],
        compiler_params=pltpu.CompilerParams(collective_id=0, has_side_effects=True),
    )(*operands)
    return result.reshape(rows, cols, slab * mid)


def solution(mesh):
    sizes = tuple(mesh.shape[name] for name in ("lat", "gx", "gy"))
    return jax.shard_map(
        partial(shards, sizes),
        mesh=mesh,
        in_specs=(
            P(("lat", "gx", "gy"), None),
            P(),
            P(),
            P(("lat", "gx"), "gy", None, None),
            P(),
            P(),
            P(),
            P(),
        ),
        out_specs=P(("lat", "gx"), "gy", None),
        check_vma=False,
    )
```

```python
from functools import partial
import math

import jax
import jax.numpy as jnp
from jax import lax
from jax.experimental import pallas as pl
from jax.experimental.pallas import tpu as pltpu
from jax.sharding import PartitionSpec as P

MESH = pl.DeviceIdType.MESH
DIRECTIONS = [(dx, dy) for dx in (-1, 0, 1) for dy in (-1, 0, 1) if (dx, dy) != (0, 0)]
BF16 = jnp.bfloat16
F32 = jnp.float32
NT = (((1,), (1,)), ((), ()))


def kernel(
    sizes, latents, w_key, w_value, queries, conv_one, bias_one, conv_two, bias_two, out,
    latents_v, wk_v, wv_v, q_pad, c1_v, b1_v, c2_v, b2_v, kv, att3, hid3, result,
    local_sem, halo_send, halo_recv, col_send, col_recv, plane_send, plane_recv, keys, values, c1_t, c2_t,
):
    n_lat, n_gx, n_gy, rows, cols, slab = sizes
    lat, gx, gy = lax.axis_index("lat"), lax.axis_index("gx"), lax.axis_index("gy")
    n_plane = n_gx * n_gy
    plane = gx * n_gy + gy
    n_row_tiles = n_lat * n_gx
    row_tile = lat * n_gx + gx
    wide = cols * slab
    edge = 2 * slab

    def device_of(tile_x, tile_y):
        return (lax.div(tile_x, n_gx), lax.rem(tile_x, n_gx), tile_y)

    def present(tile_x, tile_y):
        return (tile_x >= 0) & (tile_x < n_row_tiles) & (tile_y >= 0) & (tile_y < n_gy)

    def plane_device(index):
        return (lat, lax.div(index, n_gy), lax.rem(index, n_gy))

    loads = [
        pltpu.make_async_copy(src, dst, local_sem.at[i])
        for i, (src, dst) in enumerate([
            (latents, latents_v),
            (w_key, wk_v),
            (w_value, wv_v),
            (queries, q_pad.at[pl.ds(2, rows), pl.ds(edge, wide)]),
            (conv_one, c1_v),
            (bias_one, b1_v),
            (conv_two, c2_v),
            (bias_two, b2_v),
        ])
    ]
    for load in loads[:3]:
        load.start()

    barrier = pltpu.get_barrier_semaphore()
    awaited = n_lat - 1 + n_plane - 1
    for k in range(1, n_lat):
        pl.semaphore_signal(barrier, inc=1, device_id=(lax.rem(lat + k, n_lat), gx, gy), device_id_type=MESH)
    for k in range(1, n_plane):
        pl.semaphore_signal(barrier, inc=1, device_id=plane_device(lax.rem(plane + k, n_plane)), device_id_type=MESH)
    for dx, dy in DIRECTIONS:
        there = present(row_tile + dx, gy + dy)
        awaited = awaited + there.astype(jnp.int32)

        @pl.when(there)
        def _():
            pl.semaphore_signal(
                barrier, inc=1, device_id=device_of(row_tile + dx, gy + dy), device_id_type=MESH
            )

    for load in loads[3:]:
        load.start()
    for load in loads[:3]:
        load.wait()
    lat_rows = latents_v[...]
    key_rows = jnp.dot(lat_rows, wk_v[...], preferred_element_type=F32).astype(BF16)
    value_rows = jnp.dot(lat_rows, wv_v[...], preferred_element_type=F32).astype(BF16)
    kv[plane, lat] = jnp.concatenate([key_rows, value_rows], axis=1)

    pl.semaphore_wait(barrier, awaited)

    def column_copy(k, owner):
        slot = kv.at[plane, owner]
        return pltpu.make_async_remote_copy(
            src_ref=slot, dst_ref=slot, send_sem=col_send.at[k], recv_sem=col_recv.at[k],
            device_id=(lax.rem(lat + k, n_lat), gx, gy), device_id_type=MESH,
        )

    def plane_copy(k, owner):
        slot = kv.at[owner]
        return pltpu.make_async_remote_copy(
            src_ref=slot, dst_ref=slot, send_sem=plane_send.at[k], recv_sem=plane_recv.at[k],
            device_id=plane_device(lax.rem(plane + k, n_plane)), device_id_type=MESH,
        )

    def halo_copy(i, dx, dy):
        src_x = {1: rows - 2, -1: 0, 0: 0}[dx]
        dst_x = {1: 0, -1: rows + 2, 0: 2}[dx]
        src_y = {1: wide - edge, -1: 0, 0: 0}[dy]
        dst_y = {1: 0, -1: wide + edge, 0: edge}[dy]
        size_x, size_y = (rows if dx == 0 else 2), (wide if dy == 0 else edge)
        return pltpu.make_async_remote_copy(
            src_ref=queries.at[pl.ds(src_x, size_x), pl.ds(src_y, size_y)],
            dst_ref=q_pad.at[pl.ds(dst_x, size_x), pl.ds(dst_y, size_y)],
            send_sem=halo_send.at[i], recv_sem=halo_recv.at[i],
            device_id=device_of(row_tile + dx, gy + dy), device_id_type=MESH,
        )

    for k in range(1, n_lat):
        column_copy(k, lat).start()
    for i, (dx, dy) in enumerate(DIRECTIONS):
        @pl.when(present(row_tile + dx, gy + dy))
        def _():
            halo_copy(i, dx, dy).start()

    for k in range(1, n_lat):
        column_copy(k, lax.rem(lat + n_lat - k, n_lat)).wait_recv()
    for k in range(1, n_plane):
        plane_copy(k, plane).start()

    for load in loads[3:]:
        load.wait()
    for turned, weight in ((c1_t, c1_v), (c2_t, c2_v)):
        depth = weight.shape[2]
        for a in range(3):
            turned[a * depth : (a + 1) * depth, :] = weight[a].T
    for i, (dx, dy) in enumerate(DIRECTIONS):
        @pl.when(present(row_tile - dx, gy - dy))
        def _():
            halo_copy(i, dx, dy).wait_recv()

    for k in range(1, n_plane):
        plane_copy(k, lax.rem(plane + n_plane - k, n_plane)).wait_recv()

    n_all = n_plane * n_lat * kv.shape[2]
    channels = q_pad.shape[2]
    block = min(n_all, 256)
    piece_planes = block // (n_lat * kv.shape[2])
    for first in range(0, n_plane, piece_planes):
        every = kv[pl.ds(first, piece_planes)].reshape(block, 2 * channels)
        spot = pl.ds(first * n_lat * kv.shape[2], block)
        keys[spot, :] = every[:, :channels]
        values[spot, :channels] = every[:, channels:]
        values[spot, channels:] = jnp.ones((block, channels), BF16)
    exponent_scale = math.log2(math.e) / math.sqrt(channels)
    padded = wide + 2 * edge

    def shifted(cells):
        level = lax.broadcasted_iota(jnp.int32, cells.shape, 1)
        below = jnp.where(level == 0, 0.0, pltpu.roll(cells, 1, 1))
        above = jnp.where(level == slab - 1, 0.0, pltpu.roll(cells, slab - 1, 1))
        return below, above

    def attend(first, count):
        q = q_pad[pl.ds(first, count)].reshape(count * padded, channels)

        def fold(first_latent, state):
            spot = pl.ds(first_latent, block)
            scores = lax.dot_general(q, keys[spot, :], NT, preferred_element_type=F32)
            top = jnp.max(scores, axis=1, keepdims=True)
            if state is not None:
                top = jnp.maximum(top, state[0])
            weights = jnp.exp2((scores - top) * exponent_scale).astype(BF16)
            mixed = jnp.dot(weights, values[spot, :], preferred_element_type=F32)
            if state is not None:
                mixed = mixed + state[1] * jnp.exp2((state[0] - top) * exponent_scale)
            return top, mixed

        state = fold(0, None)
        if n_all > block:
            state = lax.fori_loop(
                1, n_all // block, lambda i, held: fold(pl.multiple_of(i * block, block), held), state
            )
        mixed = state[1]
        cells = (mixed[:, :channels] / mixed[:, channels:]).reshape(-1, slab, channels)
        below, above = shifted(cells)
        for c, part in enumerate((below, cells, above)):
            att3[pl.ds(first, count), :, c * channels : (c + 1) * channels] = (
                part.astype(BF16).reshape(count, padded, channels)
            )

    step = max(1, min(4, 1024 // n_all))
    steps = (rows + 4) // step
    if steps <= 4:
        for s in range(steps):
            attend(s * step, step)
    else:
        @pl.loop(0, steps)
        def _(s):
            attend(s * step, step)

    def blank(when, ref, index):
        @pl.when(when)
        def _():
            view = ref.at[index]
            view[...] = jnp.zeros(view.shape, ref.dtype)

    every_dim = slice(None)
    blank(row_tile == 0, att3, (pl.ds(0, 2), every_dim, every_dim))
    blank(row_tile == n_row_tiles - 1, att3, (pl.ds(rows + 2, 2), every_dim, every_dim))
    blank(gy == 0, att3, (every_dim, pl.ds(0, edge), every_dim))
    blank(gy == n_gy - 1, att3, (every_dim, pl.ds(wide + edge, edge), every_dim))

    def convolve(ref, weight, first, count, mid):
        length, depth = ref.shape[1:]
        taps = [ref[pl.ds(first + a, count)].reshape(count * length, depth) for a in range(3)]
        if depth % 128 == 0:
            taps = [jnp.concatenate(taps, axis=1)]
        total = None
        for a, cells in enumerate(taps):
            part = weight[a * depth : a * depth + cells.shape[1], :]
            term = jnp.dot(cells, part, preferred_element_type=F32)
            total = term if total is None else total + term
        total = total.reshape(count, length, 3 * mid)
        kept = length - 2 * slab
        return (
            total[:, :kept, :mid]
            + total[:, slab : slab + kept, mid : 2 * mid]
            + total[:, 2 * slab :, 2 * mid :]
        )

    mid = b1_v.shape[1]
    for first in range(0, rows + 2, 5):
        count = min(5, rows + 2 - first)
        half = (convolve(att3, c1_t, first, count, mid) + b1_v[...]) * 0.5
        cells = (half + half * jnp.tanh(half)).reshape(-1, slab, mid)
        below, above = shifted(cells)
        stacked = jnp.concatenate([below, cells, above], axis=2).astype(BF16)
        hid3[pl.ds(first, count)] = stacked.reshape(count, wide + edge, 3 * mid)

    blank(row_tile == 0, hid3, (pl.ds(0, 1), every_dim, every_dim))
    blank(row_tile == n_row_tiles - 1, hid3, (pl.ds(rows + 1, 1), every_dim, every_dim))
    blank(gy == 0, hid3, (every_dim, pl.ds(0, slab), every_dim))
    blank(gy == n_gy - 1, hid3, (every_dim, pl.ds(wide + slab, slab), every_dim))

    for first in range(0, rows, 4):
        final = convolve(hid3, c2_t, first, 4, mid) + b2_v[...]
        result[pl.ds(first * wide, 4 * wide), :mid] = final.reshape(4 * wide, mid)
    pieces = [result[pl.ds(z, rows * cols, stride=slab), :][:, :mid] for z in range(slab)]
    out[...] = jnp.concatenate(pieces, axis=1).astype(BF16)

    for k in range(1, n_lat):
        column_copy(k, lat).wait_send()
    for k in range(1, n_plane):
        plane_copy(k, plane).wait_send()
    for i, (dx, dy) in enumerate(DIRECTIONS):
        @pl.when(present(row_tile + dx, gy + dy))
        def _():
            halo_copy(i, dx, dy).wait_send()


def shards(sizes, latents, w_key, w_value, queries, conv_one, bias_one, conv_two, bias_two):
    rows, cols, slab, channels = queries.shape
    mid = conv_one.shape[2]
    n_lat, n_gx, n_gy = sizes
    piece = latents.shape[0]
    n_plane = n_gx * n_gy
    any_spec = pl.BlockSpec(memory_space=pl.ANY)
    operands = (
        latents, w_key, w_value,
        queries.reshape(rows, cols * slab, channels),
        conv_one.reshape(3, 3 * mid, 3 * channels),
        bias_one.reshape(1, mid),
        conv_two.reshape(3, 3 * mid, 3 * mid),
        bias_two.reshape(1, mid),
    )
    result = pl.pallas_call(
        partial(kernel, (n_lat, n_gx, n_gy, rows, cols, slab)),
        out_shape=pltpu.VMEM((rows * cols, slab * mid), BF16),
        in_specs=[any_spec] * 8,
        out_specs=pl.BlockSpec(memory_space=pltpu.VMEM),
        scratch_shapes=[
            pltpu.VMEM(latents.shape, BF16),
            pltpu.VMEM(w_key.shape, BF16),
            pltpu.VMEM(w_value.shape, BF16),
            pltpu.VMEM((rows + 4, (cols + 4) * slab, channels), BF16),
            pltpu.VMEM(operands[4].shape, BF16),
            pltpu.VMEM((1, mid), F32),
            pltpu.VMEM(operands[6].shape, BF16),
            pltpu.VMEM((1, mid), F32),
            pltpu.VMEM((n_plane, n_lat, piece, 2 * channels), BF16),
            pltpu.VMEM((rows + 4, (cols + 4) * slab, 3 * channels), BF16),
            pltpu.VMEM((rows + 2, (cols + 2) * slab, 3 * mid), BF16),
            pltpu.VMEM((rows * cols * slab, 2 * mid), F32),
            pltpu.SemaphoreType.DMA((8,)),
            pltpu.SemaphoreType.DMA((8,)),
            pltpu.SemaphoreType.DMA((8,)),
            pltpu.SemaphoreType.DMA((n_lat,)),
            pltpu.SemaphoreType.DMA((n_lat,)),
            pltpu.SemaphoreType.DMA((n_plane,)),
            pltpu.SemaphoreType.DMA((n_plane,)),
            pltpu.VMEM((n_plane * n_lat * piece, channels), BF16),
            pltpu.VMEM((n_plane * n_lat * piece, 2 * channels), BF16),
            pltpu.VMEM((9 * channels, 3 * mid), BF16),
            pltpu.VMEM((9 * mid, 3 * mid), BF16),
        ],
        compiler_params=pltpu.CompilerParams(collective_id=0, has_side_effects=True),
    )(*operands)
    return result.reshape(rows, cols, slab * mid)


def solution(mesh):
    sizes = tuple(mesh.shape[name] for name in ("lat", "gx", "gy"))
    return jax.shard_map(
        partial(shards, sizes),
        mesh=mesh,
        in_specs=(
            P(("lat", "gx", "gy"), None),
            P(),
            P(),
            P(("lat", "gx"), "gy", None, None),
            P(),
            P(),
            P(),
            P(),
        ),
        out_specs=P(("lat", "gx"), "gy", None),
        check_vma=False,
    )
```

```python
from functools import partial
import math

import jax
import jax.numpy as jnp
from jax import lax
from jax.experimental import pallas as pl
from jax.experimental.pallas import tpu as pltpu
from jax.sharding import PartitionSpec as P

MESH = pl.DeviceIdType.MESH
DIRECTIONS = [(dx, dy) for dx in (-1, 0, 1) for dy in (-1, 0, 1) if (dx, dy) != (0, 0)]
BF16 = jnp.bfloat16
F32 = jnp.float32
NT = (((1,), (1,)), ((), ()))


def kernel(
    sizes, latents, w_key, w_value, queries, conv_one, bias_one, conv_two, bias_two, out,
    latents_v, wk_v, wv_v, q_pad, c1_v, b1_v, c2_v, b2_v, kv, att3, hid3, result,
    local_sem, halo_send, halo_recv, col_send, col_recv, plane_send, plane_recv, keys, values, c1_t, c2_t,
):
    n_lat, n_gx, n_gy, rows, cols, slab = sizes
    lat, gx, gy = lax.axis_index("lat"), lax.axis_index("gx"), lax.axis_index("gy")
    n_plane = n_gx * n_gy
    plane = gx * n_gy + gy
    n_row_tiles = n_lat * n_gx
    row_tile = lat * n_gx + gx
    wide = cols * slab
    edge = 2 * slab

    def device_of(tile_x, tile_y):
        return (lax.div(tile_x, n_gx), lax.rem(tile_x, n_gx), tile_y)

    def present(tile_x, tile_y):
        return (tile_x >= 0) & (tile_x < n_row_tiles) & (tile_y >= 0) & (tile_y < n_gy)

    def plane_device(index):
        return (lat, lax.div(index, n_gy), lax.rem(index, n_gy))

    loads = [
        pltpu.make_async_copy(src, dst, local_sem.at[i])
        for i, (src, dst) in enumerate([
            (latents, latents_v),
            (w_key, wk_v),
            (w_value, wv_v),
            (queries, q_pad.at[pl.ds(2, rows), pl.ds(edge, wide)]),
            (conv_one, c1_v),
            (bias_one, b1_v),
            (conv_two, c2_v),
            (bias_two, b2_v),
        ])
    ]
    for load in loads[:3]:
        load.start()

    barrier = pltpu.get_barrier_semaphore()
    awaited = n_lat - 1 + n_plane - 1
    for k in range(1, n_lat):
        pl.semaphore_signal(barrier, inc=1, device_id=(lax.rem(lat + k, n_lat), gx, gy), device_id_type=MESH)
    for k in range(1, n_plane):
        pl.semaphore_signal(barrier, inc=1, device_id=plane_device(lax.rem(plane + k, n_plane)), device_id_type=MESH)
    for dx, dy in DIRECTIONS:
        if dx == 0:
            continue
        outer = 0 if dx < 0 else n_gx - 1
        there = present(row_tile + dx, gy + dy) & (gx == outer)
        awaited = awaited + there.astype(jnp.int32)

        @pl.when(there)
        def _():
            pl.semaphore_signal(
                barrier, inc=1, device_id=device_of(row_tile + dx, gy + dy), device_id_type=MESH
            )

    for load in loads[3:]:
        load.start()
    for load in loads[:3]:
        load.wait()
    lat_rows = latents_v[...]
    key_rows = jnp.dot(lat_rows, wk_v[...], preferred_element_type=F32).astype(BF16)
    value_rows = jnp.dot(lat_rows, wv_v[...], preferred_element_type=F32).astype(BF16)
    kv[plane, lat] = jnp.concatenate([key_rows, value_rows], axis=1)

    pl.semaphore_wait(barrier, awaited)

    def column_copy(k, owner):
        slot = kv.at[plane, owner]
        return pltpu.make_async_remote_copy(
            src_ref=slot, dst_ref=slot, send_sem=col_send.at[k], recv_sem=col_recv.at[k],
            device_id=(lax.rem(lat + k, n_lat), gx, gy), device_id_type=MESH,
        )

    def plane_copy(k, owner):
        slot = kv.at[owner]
        return pltpu.make_async_remote_copy(
            src_ref=slot, dst_ref=slot, send_sem=plane_send.at[k], recv_sem=plane_recv.at[k],
            device_id=plane_device(lax.rem(plane + k, n_plane)), device_id_type=MESH,
        )

    def halo_copy(i, dx, dy):
        src_x = {1: rows - 2, -1: 0, 0: 0}[dx]
        dst_x = {1: 0, -1: rows + 2, 0: 2}[dx]
        src_y = {1: wide - edge, -1: 0, 0: 0}[dy]
        dst_y = {1: 0, -1: wide + edge, 0: edge}[dy]
        size_x, size_y = (rows if dx == 0 else 2), (wide if dy == 0 else edge)
        return pltpu.make_async_remote_copy(
            src_ref=queries.at[pl.ds(src_x, size_x), pl.ds(src_y, size_y)],
            dst_ref=q_pad.at[pl.ds(dst_x, size_x), pl.ds(dst_y, size_y)],
            send_sem=halo_send.at[i], recv_sem=halo_recv.at[i],
            device_id=device_of(row_tile + dx, gy + dy), device_id_type=MESH,
        )

    for k in range(1, n_lat):
        column_copy(k, lat).start()
    for i, (dx, dy) in enumerate(DIRECTIONS):
        @pl.when(present(row_tile + dx, gy + dy))
        def _():
            halo_copy(i, dx, dy).start()

    for k in range(1, n_lat):
        column_copy(k, lax.rem(lat + n_lat - k, n_lat)).wait_recv()
    for k in range(1, n_plane):
        plane_copy(k, plane).start()

    for load in loads[3:]:
        load.wait()
    for turned, weight in ((c1_t, c1_v), (c2_t, c2_v)):
        depth = weight.shape[2]
        for a in range(3):
            turned[a * depth : (a + 1) * depth, :] = weight[a].T
    for i, (dx, dy) in enumerate(DIRECTIONS):
        @pl.when(present(row_tile - dx, gy - dy))
        def _():
            halo_copy(i, dx, dy).wait_recv()

    for k in range(1, n_lat):
        column_copy(k, lat).wait_send()
    for k in range(1, n_plane):
        plane_copy(k, plane).wait_send()
    for i, (dx, dy) in enumerate(DIRECTIONS):
        @pl.when(present(row_tile + dx, gy + dy))
        def _():
            halo_copy(i, dx, dy).wait_send()
    for k in range(1, n_plane):
        plane_copy(k, lax.rem(plane + n_plane - k, n_plane)).wait_recv()

    n_all = n_plane * n_lat * kv.shape[2]
    channels = q_pad.shape[2]
    block = min(n_all, 256)
    piece_planes = block // (n_lat * kv.shape[2])
    for first in range(0, n_plane, piece_planes):
        every = kv[pl.ds(first, piece_planes)].reshape(block, 2 * channels)
        spot = pl.ds(first * n_lat * kv.shape[2], block)
        keys[spot, :] = every[:, :channels]
        values[spot, :channels] = every[:, channels:]
        values[spot, channels:] = jnp.ones((block, channels), BF16)
    exponent_scale = math.log2(math.e) / math.sqrt(channels)
    padded = wide + 2 * edge

    def shifted(cells):
        level = lax.broadcasted_iota(jnp.int32, cells.shape, 1)
        below = jnp.where(level == 0, 0.0, pltpu.roll(cells, 1, 1))
        above = jnp.where(level == slab - 1, 0.0, pltpu.roll(cells, slab - 1, 1))
        return below, above

    def attend(first, count):
        q = q_pad[pl.ds(first, count)].reshape(count * padded, channels)

        def fold(first_latent, state):
            spot = pl.ds(first_latent, block)
            scores = lax.dot_general(q, keys[spot, :], NT, preferred_element_type=F32)
            top = jnp.max(scores, axis=1, keepdims=True)
            if state is not None:
                top = jnp.maximum(top, state[0])
            weights = jnp.exp2((scores - top) * exponent_scale).astype(BF16)
            mixed = jnp.dot(weights, values[spot, :], preferred_element_type=F32)
            if state is not None:
                mixed = mixed + state[1] * jnp.exp2((state[0] - top) * exponent_scale)
            return top, mixed

        state = fold(0, None)
        if n_all > block:
            state = lax.fori_loop(
                1, n_all // block, lambda i, held: fold(pl.multiple_of(i * block, block), held), state
            )
        mixed = state[1]
        cells = (mixed[:, :channels] / mixed[:, channels:]).reshape(-1, slab, channels)
        below, above = shifted(cells)
        for c, part in enumerate((below, cells, above)):
            att3[pl.ds(first, count), :, c * channels : (c + 1) * channels] = (
                part.astype(BF16).reshape(count, padded, channels)
            )

    step = max(1, min(4, 1024 // n_all))
    steps = (rows + 4) // step
    if steps <= 4:
        for s in range(steps):
            attend(s * step, step)
    else:
        @pl.loop(0, steps)
        def _(s):
            attend(s * step, step)

    def blank(when, ref, index):
        cells = ref[index]
        ref[index] = jnp.where(when, jnp.zeros_like(cells), cells)

    every_dim = slice(None)
    blank(row_tile == 0, att3, (pl.ds(0, 2), every_dim, every_dim))
    blank(row_tile == n_row_tiles - 1, att3, (pl.ds(rows + 2, 2), every_dim, every_dim))
    blank(gy == 0, att3, (every_dim, pl.ds(0, edge), every_dim))
    blank(gy == n_gy - 1, att3, (every_dim, pl.ds(wide + edge, edge), every_dim))

    def convolve(ref, weight, first, count, mid):
        length, depth = ref.shape[1:]
        taps = [ref[pl.ds(first + a, count)].reshape(count * length, depth) for a in range(3)]
        if depth % 128 == 0:
            taps = [jnp.concatenate(taps, axis=1)]
        total = None
        for a, cells in enumerate(taps):
            part = weight[a * depth : a * depth + cells.shape[1], :]
            term = jnp.dot(cells, part, preferred_element_type=F32)
            total = term if total is None else total + term
        total = total.reshape(count, length, 3 * mid)
        kept = length - 2 * slab
        return (
            total[:, :kept, :mid]
            + total[:, slab : slab + kept, mid : 2 * mid]
            + total[:, 2 * slab :, 2 * mid :]
        )

    mid = b1_v.shape[1]
    for first in range(0, rows + 2, 2):
        count = min(2, rows + 2 - first)
        half = (convolve(att3, c1_t, first, count, mid) + b1_v[...]) * 0.5
        cells = (half + half * jnp.tanh(half)).reshape(-1, slab, mid)
        below, above = shifted(cells)
        stacked = jnp.concatenate([below, cells, above], axis=2).astype(BF16)
        hid3[pl.ds(first, count)] = stacked.reshape(count, wide + edge, 3 * mid)

    blank(row_tile == 0, hid3, (pl.ds(0, 1), every_dim, every_dim))
    blank(row_tile == n_row_tiles - 1, hid3, (pl.ds(rows + 1, 1), every_dim, every_dim))
    blank(gy == 0, hid3, (every_dim, pl.ds(0, slab), every_dim))
    blank(gy == n_gy - 1, hid3, (every_dim, pl.ds(wide + slab, slab), every_dim))

    for first in range(0, rows, 2):
        final = convolve(hid3, c2_t, first, 2, mid) + b2_v[...]
        result[pl.ds(first * wide, 2 * wide), :mid] = final.reshape(2 * wide, mid)
    pieces = [result[pl.ds(z, rows * cols, stride=slab), :][:, :mid] for z in range(slab)]
    out[...] = jnp.concatenate(pieces, axis=1).astype(BF16)


def shards(sizes, latents, w_key, w_value, queries, conv_one, bias_one, conv_two, bias_two):
    rows, cols, slab, channels = queries.shape
    mid = conv_one.shape[2]
    n_lat, n_gx, n_gy = sizes
    piece = latents.shape[0]
    n_plane = n_gx * n_gy
    any_spec = pl.BlockSpec(memory_space=pl.ANY)
    operands = (
        latents, w_key, w_value,
        queries.reshape(rows, cols * slab, channels),
        conv_one.reshape(3, 3 * mid, 3 * channels),
        bias_one.reshape(1, mid),
        conv_two.reshape(3, 3 * mid, 3 * mid),
        bias_two.reshape(1, mid),
    )
    result = pl.pallas_call(
        partial(kernel, (n_lat, n_gx, n_gy, rows, cols, slab)),
        out_shape=pltpu.VMEM((rows * cols, slab * mid), BF16),
        in_specs=[any_spec] * 8,
        out_specs=pl.BlockSpec(memory_space=pltpu.VMEM),
        scratch_shapes=[
            pltpu.VMEM(latents.shape, BF16),
            pltpu.VMEM(w_key.shape, BF16),
            pltpu.VMEM(w_value.shape, BF16),
            pltpu.VMEM((rows + 4, (cols + 4) * slab, channels), BF16),
            pltpu.VMEM(operands[4].shape, BF16),
            pltpu.VMEM((1, mid), F32),
            pltpu.VMEM(operands[6].shape, BF16),
            pltpu.VMEM((1, mid), F32),
            pltpu.VMEM((n_plane, n_lat, piece, 2 * channels), BF16),
            pltpu.VMEM((rows + 4, (cols + 4) * slab, 3 * channels), BF16),
            pltpu.VMEM((rows + 2, (cols + 2) * slab, 3 * mid), BF16),
            pltpu.VMEM((rows * cols * slab, 2 * mid), F32),
            pltpu.SemaphoreType.DMA((8,)),
            pltpu.SemaphoreType.DMA((8,)),
            pltpu.SemaphoreType.DMA((8,)),
            pltpu.SemaphoreType.DMA((n_lat,)),
            pltpu.SemaphoreType.DMA((n_lat,)),
            pltpu.SemaphoreType.DMA((n_plane,)),
            pltpu.SemaphoreType.DMA((n_plane,)),
            pltpu.VMEM((n_plane * n_lat * piece, channels), BF16),
            pltpu.VMEM((n_plane * n_lat * piece, 2 * channels), BF16),
            pltpu.VMEM((9 * channels, 3 * mid), BF16),
            pltpu.VMEM((9 * mid, 3 * mid), BF16),
        ],
        compiler_params=pltpu.CompilerParams(collective_id=0, has_side_effects=True),
    )(*operands)
    return result.reshape(rows, cols, slab * mid)


def solution(mesh):
    sizes = tuple(mesh.shape[name] for name in ("lat", "gx", "gy"))
    return jax.shard_map(
        partial(shards, sizes),
        mesh=mesh,
        in_specs=(
            P(("lat", "gx", "gy"), None),
            P(),
            P(),
            P(("lat", "gx"), "gy", None, None),
            P(),
            P(),
            P(),
            P(),
        ),
        out_specs=P(("lat", "gx"), "gy", None),
        check_vma=False,
    )
```
